32 devices in a mesh: dp: 8 (over z, y), tensor: 4 (over x, core).
Axes of the slice: x: 2, y: 2, z: 4, core: 2. Of those that a mesh axis runs over, the one named last changes fastest.
Arguments:
- tokens: bfloat16 [8192, 1024], P(('dp', 'tensor')), may hold values from -6 to 6
- cotangent: bfloat16 [8192, 1024], P(('dp', 'tensor')), may hold values from -6 to 6
- prefix: int32 [8], P('dp'), may hold values from 102 to 512
- qkv_weight: float32 [1024, 3, 1024], P('dp', None, 'tensor'), may hold values from -0.1875 to 0.1875
- qkv_moment: float32 [1024, 3, 1024], P('dp', None, 'tensor'), may hold values from -112 to 112
- qkv_square: float32 [1024, 3, 1024], P('dp', None, 'tensor'), may hold values from 24.576 to 2457.6
- out_weight: float32 [1024, 1024], P('dp', 'tensor'), may hold values from -1 to 1
- out_moment: float32 [1024, 1024], P('dp', 'tensor'), may hold values from -112 to 112
- out_square: float32 [1024, 1024], P('dp', 'tensor'), may hold values from 24.576 to 2457.6
- up_weight: float32 [1024, 4096], P('dp', 'tensor'), may hold values from -0.1875 to 0.1875
- up_moment: float32 [1024, 4096], P('dp', 'tensor'), may hold values from -112 to 112
- up_square: float32 [1024, 4096], P('dp', 'tensor'), may hold values from 24.576 to 2457.6
- down_weight: float32 [1024, 4096], P('dp', 'tensor'), may hold values from -0.09375 to 0.09375
- down_moment: float32 [1024, 4096], P('dp', 'tensor'), may hold values from -112 to 112
- down_square: float32 [1024, 4096], P('dp', 'tensor'), may hold values from 24.576 to 2457.6
- norm_gains: float32 [2, 1024], replicated, may hold values from 0.5 to 1.5
- gains_moment: float32 [2, 1024], replicated, may hold values from -256 to 256
- gains_square: float32 [2, 1024], replicated, may hold values from 245.76 to 8192
- biases: float32 [6, 1024], replicated, may hold values from -1.75 to 1.75
- biases_moment: float32 [6, 1024], replicated, may hold values from -256 to 256
- biases_square: float32 [6, 1024], replicated, may hold values from 8192 to 819200
- up_bias: float32 [4096], replicated, may hold values from -1.75 to 1.75
- up_bias_moment: float32 [4096], replicated, may hold values from -256 to 256
- up_bias_square: float32 [4096], replicated, may hold values from 245.76 to 8192
Outputs:
- output: bfloat16 [8192, 1024], P(('dp', 'tensor'))
- input_grad: float32 [8192, 1024], P(('dp', 'tensor'))
- qkv_weight_grad: float32 [1024, 3, 1024], P('dp', None, 'tensor')
- out_weight_grad: float32 [1024, 1024], P('dp', 'tensor')
- up_weight_grad: float32 [1024, 4096], P('dp', 'tensor')
- down_weight_grad: float32 [1024, 4096], P('dp', 'tensor')
- norm_gains_grad: float32 [2, 1024], replicated
- biases_grad: float32 [6, 1024], replicated
- up_bias_grad: float32 [4096], replicated
- qkv_weight_new: float32 [1024, 3, 1024], P('dp', None, 'tensor')
- out_weight_new: float32 [1024, 1024], P('dp', 'tensor')
- up_weight_new: float32 [1024, 4096], P('dp', 'tensor')
- down_weight_new: float32 [1024, 4096], P('dp', 'tensor')
- norm_gains_new: float32 [2, 1024], replicated
- biases_new: float32 [6, 1024], replicated
- up_bias_new: float32 [4096], replicated
- qkv_weight_low: bfloat16 [1024, 3, 1024], P('dp', None, 'tensor')
- out_weight_low: bfloat16 [1024, 1024], P('dp', 'tensor')
- up_weight_low: bfloat16 [1024, 4096], P('dp', 'tensor')
- down_weight_low: bfloat16 [1024, 4096], P('dp', 'tensor')
- qkv_moment_new: float32 [1024, 3, 1024], P('dp', None, 'tensor')
- out_moment_new: float32 [1024, 1024], P('dp', 'tensor')
- up_moment_new: float32 [1024, 4096], P('dp', 'tensor')
- down_moment_new: float32 [1024, 4096], P('dp', 'tensor')
- gains_moment_new: float32 [2, 1024], replicated
- biases_moment_new: float32 [6, 1024], replicated
- up_bias_moment_new: float32 [4096], replicated
- qkv_square_new: float32 [1024, 3, 1024], P('dp', None, 'tensor')
- out_square_new: float32 [1024, 1024], P('dp', 'tensor')
- up_square_new: float32 [1024, 4096], P('dp', 'tensor')
- down_square_new: float32 [1024, 4096], P('dp', 'tensor')
- gains_square_new: float32 [2, 1024], replicated
- biases_square_new: float32 [6, 1024], replicated
- up_bias_square_new: float32 [4096], replicated
- weight_norms: float32 [4], replicated
- step_norms: float32 [4], replicated
The draws below stay inside these ranges and needn't reach their ends.
All inputs are finite; a program needn't handle non-finite values.
Results may differ from the reference program's by a relative error of at most 0.022.
Values may be sent and summed in bfloat16 or wider, within the bound.
No kernel may reach another device: no remote copies, remote signals or barrier semaphores. Data moves between devices by JAX's collectives and lax.ppermute only.
A program may use at most 128 MiB of HBM per device.

```python
import math
import jax
import jax.numpy as jnp
from jax import lax

D = 1024
HEADS = 16
HEAD = 64
FF = 4096
QBLOCK = 512
SEQ_LEN = 1024
SEQS = 8
TOKENS = 8192


def place_ends(array, stream_key, least, largest):
    longest = array.shape.index(max(array.shape))
    spots = []
    for shift in (0, 1):
        where = [jax.random.randint(jax.random.fold_in(stream_key, axis), (), 0, length) for axis, length in enumerate(array.shape)]
        where[longest] = (where[longest] + shift) % array.shape[longest]
        spots.append(tuple(where))
    return array.at[spots[0]].set(least).at[spots[1]].set(largest)


def level_of(rng, shape, split, least, largest):
    def one(axis_at, parts):
        steps = jax.random.uniform(jax.random.fold_in(jax.random.fold_in(rng, 6), axis_at), (parts,), jnp.float32, least / len(split), largest / len(split))
        return jnp.repeat(jnp.exp(steps), shape[axis_at] // parts).reshape((-1,) + (1,) * (len(shape) - axis_at - 1))

    factor_of = one(*split[0])
    for cut in split[1:]:
        factor_of = factor_of * one(*cut)
    return factor_of


def normal_values(key, dims, spread, limit, split=(), held_as=jnp.bfloat16):
    level = level_of(key, dims, split, -0.22, 0.18) if split else 1.0
    array = jax.random.normal(key, dims, jnp.float32) * spread * level
    return jnp.minimum(jnp.maximum(array, -limit), limit).astype(held_as)


def setup_inputs(seed: int = 0) -> dict:
    key_of = jax.random.split(jax.random.key(seed), 25)
    return {
        "tokens": normal_values(key_of[0], (TOKENS, D), 1.0, 6.0, ((0, 32),)),
        "cotangent": normal_values(key_of[1], (TOKENS, D), 1.0, 6.0, ((0, 32),)),
        "prefix": place_ends(jax.random.randint(key_of[2], (SEQS,), SEQ_LEN // 10, SEQ_LEN // 2 + 1), jax.random.fold_in(key_of[2], 1), SEQ_LEN // 10, (SEQ_LEN // 2 + 1) - 1).astype(jnp.int32),
        "qkv_weight": normal_values(key_of[3], (D, 3, D), D ** -0.5, 0.1875, ((0, 8), (2, 4)), jnp.float32),
        "qkv_moment": normal_values(key_of[4], (D, 3, D), (0.2 * TOKENS ** 0.5), 112.0, ((0, 8), (2, 4)), jnp.float32),
        "qkv_square": jnp.clip(jnp.exp(math.log(2457.6) - 4.6051702 * jax.random.uniform(key_of[5], (D, 3, D), jnp.float32) ** level_of(key_of[5], (D, 3, D), ((0, 8), (2, 4)), -0.2, 0.2)), 24.576, 2457.6),
        "out_weight": normal_values(key_of[6], (D, D), (D // 32) ** -0.5, 1.0, ((0, 8), (1, 4)), jnp.float32),
        "out_moment": normal_values(key_of[7], (D, D), (0.2 * TOKENS ** 0.5), 112.0, ((0, 8), (1, 4)), jnp.float32),
        "out_square": jnp.clip(jnp.exp(math.log(2457.6) - 4.6051702 * jax.random.uniform(key_of[8], (D, D), jnp.float32) ** level_of(key_of[8], (D, D), ((0, 8), (1, 4)), -0.2, 0.2)), 24.576, 2457.6),
        "up_weight": normal_values(key_of[9], (D, FF), D ** -0.5, 0.1875, ((0, 8), (1, 4)), jnp.float32),
        "up_moment": normal_values(key_of[10], (D, FF), (0.2 * TOKENS ** 0.5), 112.0, ((0, 8), (1, 4)), jnp.float32),
        "up_square": jnp.clip(jnp.exp(math.log(2457.6) - 4.6051702 * jax.random.uniform(key_of[11], (D, FF), jnp.float32) ** level_of(key_of[11], (D, FF), ((0, 8), (1, 4)), -0.2, 0.2)), 24.576, 2457.6),
        "down_weight": normal_values(key_of[12], (D, FF), FF ** -0.5, 0.09375, ((0, 8), (1, 4)), jnp.float32),
        "down_moment": normal_values(key_of[13], (D, FF), (0.2 * TOKENS ** 0.5), 112.0, ((0, 8), (1, 4)), jnp.float32),
        "down_square": jnp.clip(jnp.exp(math.log(2457.6) - 4.6051702 * jax.random.uniform(key_of[14], (D, FF), jnp.float32) ** level_of(key_of[14], (D, FF), ((0, 8), (1, 4)), -0.2, 0.2)), 24.576, 2457.6),
        "norm_gains": jnp.clip(1.0 + 0.1 * jax.random.normal(key_of[15], (2, D), jnp.float32), 0.5, 1.5),
        "gains_moment": normal_values(key_of[16], (2, D), (0.5 * TOKENS ** 0.5), 256.0, (), jnp.float32),
        "gains_square": jnp.clip(jnp.exp(jax.random.uniform(key_of[17], (2, D), jnp.float32, math.log(245.76), math.log(8192.0))), 245.76, 8192.0),
        "biases": normal_values(key_of[18], (6, D), 0.3, 1.75, (), jnp.float32),
        "biases_moment": normal_values(key_of[19], (6, D), (0.5 * TOKENS ** 0.5), 256.0, (), jnp.float32),
        "biases_square": jnp.clip(jnp.exp(jax.random.uniform(key_of[20], (6, D), jnp.float32, math.log(8192.0), math.log(819200.0))), 8192.0, 819200.0),
        "up_bias": normal_values(key_of[21], (FF,), 0.3, 1.75, (), jnp.float32),
        "up_bias_moment": normal_values(key_of[22], (FF,), (0.5 * TOKENS ** 0.5), 256.0, (), jnp.float32),
        "up_bias_square": jnp.clip(jnp.exp(jax.random.uniform(key_of[23], (FF,), jnp.float32, math.log(245.76), math.log(8192.0))), 245.76, 8192.0),
    }


highest = lax.Precision.HIGHEST
learn_rate = 0.5

@jax.custom_vjp
def low(v):
    return lax.optimization_barrier(v.astype(jnp.bfloat16)).astype(jnp.float32)

@jax.custom_vjp
def low_back(v):
    return v

def low_keep(v):
    return (low(v), None)

def low_pass(kept, grad):
    return (grad,)

def back_keep(v):
    return (v, None)

def back_low(kept, grad):
    return (low(grad),)
low.defvjp(low_keep, low_pass)
low_back.defvjp(back_keep, back_low)

def layer_norm(values, gain, shift):
    mean = lax.optimization_barrier(jnp.mean(values, axis=-1, keepdims=True))
    centred = values - mean
    inverse = lax.rsqrt(lax.optimization_barrier(jnp.mean(centred * centred, axis=-1, keepdims=True)) + 1e-05)
    return centred * inverse * gain + shift

def gelu_value(v):
    return 0.5 * v * (1.0 + jnp.tanh(0.7978845608028654 * (v + 0.044715 * v * v * v)))

def alibi_slopes():
    return jnp.exp2(-8.0 * (lax.iota(jnp.int32, HEADS) + 1).astype(jnp.float32) / HEADS)

def sequence_out(x, prefix_len, qkv, outw, upw, downw, gains, shifts, upb):
    length = x.shape[0]
    block = min(QBLOCK, length)
    scale = float(HEAD) ** (-0.5)
    normed = low(layer_norm(x, gains[0], shifts[0]))
    projected = jnp.einsum('ld,dce->cle', normed, qkv, precision=highest)
    queries = low_back(low(projected[0] + shifts[2])).reshape(length, HEADS, HEAD)
    keys = low_back(low(projected[1])).reshape(length, HEADS, HEAD)
    values = low_back(low(projected[2] + shifts[3])).reshape(length, HEADS, HEAD)
    slope = alibi_slopes()

    def attend(start):
        part = lax.dynamic_slice_in_dim(queries, start, block, 0)
        scores = jnp.einsum('bhe,khe->hbk', part, keys, precision=highest) * scale
        row_pos = start + lax.iota(jnp.int32, block)
        col_pos = lax.iota(jnp.int32, length)
        offset = (col_pos[None, :] - row_pos[:, None]).astype(jnp.float32)
        scores = low_back(scores + slope[:, None, None] * offset[None])
        allowed = (col_pos[None, :] <= row_pos[:, None]) | (col_pos[None, :] < prefix_len)
        probs = jax.nn.softmax(jnp.where(allowed[None], scores, -1e+30), axis=-1)
        return jnp.einsum('hbk,khe->bhe', low(probs), values, precision=highest)
    starts = lax.iota(jnp.int32, length // block) * block
    context = lax.map(jax.checkpoint(attend), starts).reshape(length, HEADS * HEAD)
    context = low_back(low(context))
    attn = jnp.dot(context, outw.T, precision=highest) + shifts[4]
    resid = x + low_back(attn)
    normed_two = low(layer_norm(resid, gains[1], shifts[1]))
    pre = low_back(jnp.dot(normed_two, upw, precision=highest) + upb)
    hidden = low(gelu_value(pre))
    mlp = low_back(jnp.dot(hidden, downw.T, precision=highest) + shifts[5])
    return resid + mlp

def adam_terms(moment, square, grad):
    new_moment = 0.5 * moment + 0.5 * grad
    new_square = 0.5 * square + 0.5 * grad * grad
    return (new_moment, new_square, new_moment / (jnp.sqrt(new_square) + 1e-06))

def lamb_matrix(weight, moment, square, grad):
    new_moment, new_square, direction = adam_terms(moment, square, grad)
    weight_norm = jnp.sqrt(jnp.sum(weight * weight))
    step_norm = jnp.sqrt(jnp.sum(direction * direction))
    new_weight = weight - learn_rate * (weight_norm / step_norm) * direction
    return (new_weight, new_moment, new_square, weight_norm, step_norm)

def lamb_rows(weight, moment, square, grad):
    new_moment, new_square, direction = adam_terms(moment, square, grad)
    weight_norm = jnp.sqrt(lax.optimization_barrier(jnp.sum(weight * weight, axis=-1, keepdims=True)))
    step_norm = jnp.sqrt(lax.optimization_barrier(jnp.sum(direction * direction, axis=-1, keepdims=True)))
    new_weight = weight - learn_rate * (weight_norm / step_norm) * direction
    return (new_weight, new_moment, new_square)

def reference(tokens, cotangent, prefix, qkv_weight, qkv_moment, qkv_square, out_weight, out_moment, out_square, up_weight, up_moment, up_square, down_weight, down_moment, down_square, norm_gains, gains_moment, gains_square, biases, biases_moment, biases_square, up_bias, up_bias_moment, up_bias_square):
    mats = (low(qkv_weight), low(out_weight), low(up_weight), low(down_weight))
    small = (norm_gains, biases, up_bias)
    xs = tokens.astype(jnp.float32).reshape(SEQS, SEQ_LEN, D)
    cs = cotangent.astype(jnp.float32).reshape(SEQS, SEQ_LEN, D)

    def one(carry, item):
        x, cot, prefix_len = item

        def forward(xx, qkv, outw, upw, downw, gains, shifts, upb):
            return sequence_out(xx, prefix_len, qkv, outw, upw, downw, gains, shifts, upb)
        result, pull = jax.vjp(forward, x, *mats, *small)
        grads = pull(cot)
        carry = tuple((a + b for a, b in zip(carry, grads[1:])))
        return (carry, (result.astype(jnp.bfloat16), grads[0]))
    zero = tuple((jnp.zeros_like(p) for p in mats + small))
    totals, (outs, dxs) = lax.scan(one, zero, (xs, cs, prefix))
    qkv_g, out_g, up_g, down_g, gains_g, biases_g, upb_g = totals
    qkv_n, qkv_m, qkv_s, qkv_wn, qkv_sn = lamb_matrix(qkv_weight, qkv_moment, qkv_square, qkv_g)
    out_n, out_m, out_s, out_wn, out_sn = lamb_matrix(out_weight, out_moment, out_square, out_g)
    up_n, up_m, up_s, up_wn, up_sn = lamb_matrix(up_weight, up_moment, up_square, up_g)
    down_n, down_m, down_s, down_wn, down_sn = lamb_matrix(down_weight, down_moment, down_square, down_g)
    gains_n, gains_m, gains_s = lamb_rows(norm_gains, gains_moment, gains_square, gains_g)
    biases_n, biases_m, biases_s = lamb_rows(biases, biases_moment, biases_square, biases_g)
    upb_n, upb_m, upb_s = lamb_rows(up_bias, up_bias_moment, up_bias_square, upb_g)
    weight_norms = jnp.stack([qkv_wn, out_wn, up_wn, down_wn])
    step_norms = jnp.stack([qkv_sn, out_sn, up_sn, down_sn])
    return (outs.reshape(TOKENS, D), dxs.reshape(TOKENS, D), qkv_g, out_g, up_g, down_g, gains_g, biases_g, upb_g, qkv_n, out_n, up_n, down_n, gains_n, biases_n, upb_n, qkv_n.astype(jnp.bfloat16), out_n.astype(jnp.bfloat16), up_n.astype(jnp.bfloat16), down_n.astype(jnp.bfloat16), qkv_m, out_m, up_m, down_m, gains_m, biases_m, upb_m, qkv_s, out_s, up_s, down_s, gains_s, biases_s, upb_s, weight_norms, step_norms)
```

```python
import jax
import jax.numpy as jnp
from jax import lax
from jax.sharding import PartitionSpec as P

HEADS = 16
HEAD = 64


learn_rate = 0.5
gelu_coef = 0.7978845608028654


def norm_forward(values, gain, shift):
    mean = jnp.mean(values, axis=-1, keepdims=True)
    centred = values - mean
    inverse = lax.rsqrt(jnp.mean(centred * centred, axis=-1, keepdims=True) + 1e-05)
    unit = centred * inverse
    return (unit * gain + shift, unit, inverse)


def norm_backward(grad, unit, inverse, gain):
    scaled = grad * gain
    inner = (
        scaled
        - jnp.mean(scaled, axis=-1, keepdims=True)
        - unit * jnp.mean(scaled * unit, axis=-1, keepdims=True)
    )
    return (inverse * inner, jnp.sum(grad * unit, axis=0), jnp.sum(grad, axis=0))


def gelu_value(v):
    return 0.5 * v * (1.0 + jnp.tanh(gelu_coef * (v + 0.044715 * v * v * v)))


def gelu_slope(v):
    hyper = jnp.tanh(gelu_coef * (v + 0.044715 * v * v * v))
    return 0.5 * (1.0 + hyper) + 0.5 * v * (1.0 - hyper * hyper) * gelu_coef * (
        1.0 + 3.0 * 0.044715 * v * v
    )


def alibi_slopes():
    return jnp.exp2(-8.0 * (lax.iota(jnp.int32, HEADS) + 1).astype(jnp.float32) / HEADS)


def swap(v, axis, rel):
    return lax.ppermute(v, axis, [(i, i ^ rel) for i in range(lax.axis_size(axis))])


def dp_split():
    bits = lax.axis_size("dp").bit_length() - 1
    low = 1 << ((bits - 1) // 2)
    return lax.axis_size("dp") // low, low


def dp_order():
    high, low = dp_split()
    return [major * low + minor for minor in range(low) for major in range(high)]


def to_relative(v, me):
    width = v.shape[-1] // lax.axis_size("dp")
    return jnp.concatenate(
        [lax.dynamic_slice_in_dim(v, (me ^ rel) * width, width, v.ndim - 1) for rel in dp_order()],
        axis=-1,
    )


def from_relative(v, me):
    order = dp_order()
    width = v.shape[-1] // len(order)
    spot = jnp.asarray([order.index(rel) for rel in range(len(order))], jnp.int32)
    return jnp.concatenate(
        [
            lax.dynamic_slice_in_dim(v, spot[me ^ block] * width, width, v.ndim - 1)
            for block in range(len(order))
        ],
        axis=-1,
    )


def gather_rows(shard):
    high, low = dp_split()
    pieces = {0: shard}
    for major in range(1, high):
        pieces[major * low] = swap(shard, "dp", major * low)
    for minor in range(1, low):
        for major in range(high):
            pieces[major * low + minor] = swap(pieces[major * low], "dp", minor)
    return jnp.concatenate([pieces[rel] for rel in dp_order()], axis=0)


def scatter_rows(parts):
    high, low = dp_split()
    rows = parts[0].shape[0] // high
    total = parts[0].astype(jnp.float32)
    for minor in range(1, low):
        total = total + swap(parts[minor].astype(jnp.bfloat16), "dp", minor).astype(jnp.float32)
    result = total[:rows]
    low_total = total.astype(jnp.bfloat16)
    for major in range(1, high):
        block = low_total[major * rows : (major + 1) * rows]
        result = result + swap(block, "dp", major * low).astype(jnp.float32)
    return result


def share_rows(own):
    count = lax.axis_size("tensor")
    pieces = {0: own, 1: swap(own, "tensor", 1)}
    for rel in range(2, count, 2):
        pieces[rel] = swap(own, "tensor", rel)
        pieces[rel + 1] = swap(pieces[rel], "tensor", 1)
    return [pieces[rel] for rel in range(count)]


def collect_rows(blocks):
    total = blocks[0].astype(jnp.float32)
    for rel in range(2, len(blocks), 2):
        other = swap(blocks[rel + 1].astype(jnp.bfloat16), "tensor", 1).astype(jnp.float32)
        joined = (blocks[rel].astype(jnp.float32) + other).astype(jnp.bfloat16)
        total = total + swap(joined, "tensor", rel).astype(jnp.float32)
    return total + swap(blocks[1].astype(jnp.bfloat16), "tensor", 1).astype(jnp.float32)


def sum_everywhere(v):
    for axis in ("tensor", "dp"):
        total = v
        for rel in range(1, lax.axis_size(axis)):
            total = total + swap(v, axis, rel)
        v = total
    return v


def place(part, width, rank):
    return lax.dynamic_update_slice(jnp.zeros((width,), jnp.float32), part, (rank * part.shape[0],))


def adam_terms(moment, square, grad):
    new_moment = 0.5 * moment + 0.5 * grad
    new_square = 0.5 * square + 0.5 * grad * grad
    return (new_moment, new_square, new_moment / (jnp.sqrt(new_square) + 1e-06))


def lamb_rows(weight, moment, square, grad):
    new_moment, new_square, direction = adam_terms(moment, square, grad)
    weight_norm = jnp.sqrt(jnp.sum(weight * weight, axis=-1, keepdims=True))
    step_norm = jnp.sqrt(jnp.sum(direction * direction, axis=-1, keepdims=True))
    return (weight - learn_rate * (weight_norm / step_norm) * direction, new_moment, new_square)


def per_device(
    tokens,
    cotangent,
    prefix,
    qkv_weight,
    qkv_moment,
    qkv_square,
    out_weight,
    out_moment,
    out_square,
    up_weight,
    up_moment,
    up_square,
    down_weight,
    down_moment,
    down_square,
    norm_gains,
    gains_moment,
    gains_square,
    biases,
    biases_moment,
    biases_square,
    up_bias,
    up_bias_moment,
    up_bias_square,
):
    rows = tokens.shape[0]
    count = lax.axis_size("tensor")
    length = rows * count
    rank = lax.axis_index("tensor")
    me = lax.axis_index("dp")
    local_width = qkv_weight.shape[2]
    local_hidden = up_weight.shape[1]
    heads_here = local_width // HEAD
    scale = float(HEAD) ** (-0.5)
    prefix_len = prefix[0]
    slope = lax.dynamic_slice_in_dim(alibi_slopes(), rank * heads_here, heads_here)
    vectors = to_relative(
        jnp.stack([norm_gains[0], norm_gains[1], biases[0], biases[1], biases[4], biases[5]]), me
    )
    x_rows = to_relative(tokens, me).astype(jnp.float32)
    cot = to_relative(cotangent, me)
    qkv_full = gather_rows(qkv_weight.astype(jnp.bfloat16).reshape(-1, 3 * local_width))
    normed, unit_one, inverse_one = norm_forward(x_rows, vectors[0], vectors[2])
    normed_blocks = share_rows(normed.astype(jnp.bfloat16))
    normed_all = jnp.concatenate(normed_blocks, axis=0)
    out_full = gather_rows(out_weight.astype(jnp.bfloat16))
    up_full = gather_rows(up_weight.astype(jnp.bfloat16))
    down_full = gather_rows(down_weight.astype(jnp.bfloat16))
    cot_blocks = share_rows(cot)
    projected = jnp.dot(normed_all, qkv_full, preferred_element_type=jnp.float32)
    query_bias = lax.dynamic_slice_in_dim(biases[2], rank * local_width, local_width)
    value_bias = lax.dynamic_slice_in_dim(biases[3], rank * local_width, local_width)
    queries = (projected[:, :local_width] + query_bias).astype(jnp.bfloat16)
    keys = projected[:, local_width : 2 * local_width].astype(jnp.bfloat16)
    values = (projected[:, 2 * local_width :] + value_bias).astype(jnp.bfloat16)
    heads = lambda v: v.reshape(-1, heads_here, HEAD)
    position = jnp.concatenate(
        [(rank ^ rel) * rows + lax.iota(jnp.int32, rows) for rel in range(count)]
    )

    def scores_of(part, start):
        spots = position[start : start + part.shape[0]]
        scores = (
            jnp.einsum("bhe,khe->hbk", heads(part), heads(keys), preferred_element_type=jnp.float32)
            * scale
        )
        offset = (position[None, :] - spots[:, None]).astype(jnp.float32)
        allowed = (position[None, :] <= spots[:, None]) | (position[None, :] < prefix_len)
        return jnp.where(allowed[None], scores + slope[:, None, None] * offset[None], -1e30)

    half = 2 * rows
    order = list(range(length - half, -1, -half))
    logsum, context, attn_blocks = {}, {}, {}
    for start in order:
        scores = scores_of(queries[start : start + half], start)
        peak = jnp.max(scores, axis=-1, keepdims=True)
        expo = jnp.exp(scores - peak)
        totals = jnp.sum(expo, axis=-1, keepdims=True)
        logsum[start] = peak + jnp.log(totals)
        probs = (expo / totals).astype(jnp.bfloat16)
        mixed = jnp.einsum("hbk,khe->bhe", probs, heads(values), preferred_element_type=jnp.float32)
        context[start] = mixed.reshape(half, local_width).astype(jnp.bfloat16)
        part = jnp.einsum("le,de->ld", context[start], out_full, preferred_element_type=jnp.float32)
        part = part.astype(jnp.bfloat16)
        attn_blocks[start // rows], attn_blocks[start // rows + 1] = part[:rows], part[rows:]
    attn_rows = collect_rows([attn_blocks[rel] for rel in range(count)])
    resid = x_rows + (attn_rows + vectors[4])
    normed_two, unit_two, inverse_two = norm_forward(resid, vectors[1], vectors[3])
    two_blocks = share_rows(normed_two.astype(jnp.bfloat16))
    up_slice = lax.dynamic_slice_in_dim(up_bias, rank * local_hidden, local_hidden)
    hidden, pre_grads, two_grads, mlp_blocks, up_bias_sum = {}, {}, {}, {}, 0.0
    for start in range(0, count, 2):
        two = jnp.concatenate(two_blocks[start : start + 2], axis=0)
        cot_two = jnp.concatenate(cot_blocks[start : start + 2], axis=0)
        pre = jnp.dot(two, up_full, preferred_element_type=jnp.float32) + up_slice
        hidden[start] = gelu_value(pre).astype(jnp.bfloat16)
        hidden_grad = jnp.dot(cot_two, down_full, preferred_element_type=jnp.float32)
        pre_grads[start] = (hidden_grad * gelu_slope(pre)).astype(jnp.bfloat16)
        up_bias_sum = up_bias_sum + jnp.sum(pre_grads[start], axis=0, dtype=jnp.float32)
        part = jnp.einsum("lf,df->ld", pre_grads[start], up_full, preferred_element_type=jnp.float32)
        part = part.astype(jnp.bfloat16)
        two_grads[start], two_grads[start + 1] = part[:rows], part[rows:]
    two_grad = collect_rows([two_grads[rel] for rel in range(count)])
    hidden_all = jnp.concatenate([hidden[start] for start in range(0, count, 2)], axis=0)
    pre_grad_all = jnp.concatenate([pre_grads[start] for start in range(0, count, 2)], axis=0)
    two_all = jnp.concatenate(two_blocks, axis=0)
    cot_all = jnp.concatenate(cot_blocks, axis=0)
    low = dp_split()[1]

    def weight_parts(left, right):
        width = left.shape[1] // low
        return [
            jnp.einsum(
                "ld,lf->df",
                left[:, minor * width : (minor + 1) * width],
                right,
                preferred_element_type=jnp.float32,
            )
            for minor in range(low)
        ]

    down_g = scatter_rows(weight_parts(cot_all, hidden_all))
    up_g = scatter_rows(weight_parts(two_all, pre_grad_all))
    mlp = jnp.einsum("lf,df->ld", hidden_all, down_full, preferred_element_type=jnp.float32)
    mlp = mlp.astype(jnp.bfloat16)
    mlp_rows = collect_rows([mlp[rel * rows : (rel + 1) * rows] for rel in range(count)])
    output = from_relative((resid + (mlp_rows + vectors[5])).astype(jnp.bfloat16), me)
    out_grad = cot.astype(jnp.float32)
    down_bias_part = jnp.sum(out_grad, axis=0)
    resid_from_norm, gain_two_part, shift_two_part = norm_backward(
        two_grad, unit_two, inverse_two, vectors[1]
    )
    resid_grad = out_grad + resid_from_norm
    branch_low = resid_grad.astype(jnp.bfloat16)
    out_bias_part = jnp.sum(branch_low, axis=0, dtype=jnp.float32)
    branch_blocks = share_rows(branch_low)
    key_grad, value_grad, query_low = 0.0, 0.0, {}
    for start in order[::-1]:
        branch = jnp.concatenate(branch_blocks[start // rows : start // rows + 2], axis=0)
        grad_out = jnp.dot(branch, out_full, preferred_element_type=jnp.float32)
        grad_out = heads(grad_out.astype(jnp.bfloat16))
        part = queries[start : start + half]
        probs = jnp.exp(scores_of(part, start) - logsum[start])
        prob_grad = jnp.einsum(
            "bhe,khe->hbk", grad_out, heads(values), preferred_element_type=jnp.float32
        )
        delta = jnp.sum(probs * prob_grad, axis=-1, keepdims=True)
        score_grad = (probs * (prob_grad - delta)).astype(jnp.bfloat16)
        query_grad = jnp.einsum(
            "hbk,khe->bhe", score_grad, heads(keys), preferred_element_type=jnp.float32
        )
        query_low[start] = (query_grad * scale).reshape(half, local_width).astype(jnp.bfloat16)
        key_grad = key_grad + scale * jnp.einsum(
            "hbk,bhe->khe", score_grad, heads(part), preferred_element_type=jnp.float32
        )
        value_grad = value_grad + jnp.einsum(
            "hbk,bhe->khe", probs.astype(jnp.bfloat16), grad_out, preferred_element_type=jnp.float32
        )
    query_all = jnp.concatenate([query_low[start] for start in order[::-1]], axis=0)
    stacked = jnp.concatenate(
        [
            query_all,
            key_grad.reshape(length, local_width).astype(jnp.bfloat16),
            value_grad.reshape(length, local_width).astype(jnp.bfloat16),
        ],
        axis=1,
    )
    one_part = jnp.einsum("le,de->ld", stacked, qkv_full, preferred_element_type=jnp.float32)
    one_part = one_part.astype(jnp.bfloat16)
    qkv_g = scatter_rows(weight_parts(normed_all, stacked)).reshape(qkv_weight.shape)
    one_grad = collect_rows([one_part[rel * rows : (rel + 1) * rows] for rel in range(count)])
    branch_all = jnp.concatenate(branch_blocks, axis=0)
    context_all = jnp.concatenate([context[start] for start in order[::-1]], axis=0)
    out_g = scatter_rows(weight_parts(branch_all, context_all))
    input_from_norm, gain_one_part, shift_one_part = norm_backward(
        one_grad, unit_one, inverse_one, vectors[0]
    )
    input_grad = from_relative(resid_grad + input_from_norm, me)
    width = biases.shape[1]
    features = from_relative(
        jnp.stack(
            [
                gain_one_part,
                gain_two_part,
                shift_one_part,
                shift_two_part,
                out_bias_part,
                down_bias_part,
            ]
        ),
        me,
    )
    head_sums = jnp.sum(stacked, axis=0, dtype=jnp.float32)
    small = jnp.concatenate(
        [
            features.reshape(-1),
            place(head_sums[:local_width], width, rank),
            place(head_sums[2 * local_width :], width, rank),
            place(up_bias_sum, up_bias.shape[0], rank),
        ]
    )
    small = sum_everywhere(small.reshape(-1, width))
    gains_g = small[0:2]
    biases_g = jnp.concatenate([small[2:4], small[6:8], small[4:6]], axis=0)
    upb_g = small[8:].reshape(-1)
    qkv_m, qkv_s, qkv_dir = adam_terms(qkv_moment, qkv_square, qkv_g)
    out_m, out_s, out_dir = adam_terms(out_moment, out_square, out_g)
    up_m, up_s, up_dir = adam_terms(up_moment, up_square, up_g)
    down_m, down_s, down_dir = adam_terms(down_moment, down_square, down_g)
    local_sums = jnp.stack(
        [
            jnp.sum(qkv_weight * qkv_weight),
            jnp.sum(qkv_dir * qkv_dir),
            jnp.sum(out_weight * out_weight),
            jnp.sum(out_dir * out_dir),
            jnp.sum(up_weight * up_weight),
            jnp.sum(up_dir * up_dir),
            jnp.sum(down_weight * down_weight),
            jnp.sum(down_dir * down_dir),
        ]
    )
    totals = sum_everywhere(local_sums)
    norms = jnp.sqrt(totals).reshape(4, 2)
    qkv_n = qkv_weight - learn_rate * (norms[0, 0] / norms[0, 1]) * qkv_dir
    out_n = out_weight - learn_rate * (norms[1, 0] / norms[1, 1]) * out_dir
    up_n = up_weight - learn_rate * (norms[2, 0] / norms[2, 1]) * up_dir
    down_n = down_weight - learn_rate * (norms[3, 0] / norms[3, 1]) * down_dir
    gains_n, gains_m, gains_s = lamb_rows(norm_gains, gains_moment, gains_square, gains_g)
    biases_n, biases_m, biases_s = lamb_rows(biases, biases_moment, biases_square, biases_g)
    upb_n, upb_m, upb_s = lamb_rows(up_bias, up_bias_moment, up_bias_square, upb_g)
    return (
        output,
        input_grad,
        qkv_g,
        out_g,
        up_g,
        down_g,
        gains_g,
        biases_g,
        upb_g,
        qkv_n,
        out_n,
        up_n,
        down_n,
        gains_n,
        biases_n,
        upb_n,
        qkv_n.astype(jnp.bfloat16),
        out_n.astype(jnp.bfloat16),
        up_n.astype(jnp.bfloat16),
        down_n.astype(jnp.bfloat16),
        qkv_m,
        out_m,
        up_m,
        down_m,
        gains_m,
        biases_m,
        upb_m,
        qkv_s,
        out_s,
        up_s,
        down_s,
        gains_s,
        biases_s,
        upb_s,
        norms[:, 0],
        norms[:, 1],
    )


def solution(mesh):
    return jax.shard_map(
        per_device,
        mesh=mesh,
        in_specs=(
            P(("dp", "tensor"), None),
            P(("dp", "tensor"), None),
            P("dp"),
            P("dp", None, "tensor"),
            P("dp", None, "tensor"),
            P("dp", None, "tensor"),
            P("dp", "tensor"),
            P("dp", "tensor"),
            P("dp", "tensor"),
            P("dp", "tensor"),
            P("dp", "tensor"),
            P("dp", "tensor"),
            P("dp", "tensor"),
            P("dp", "tensor"),
            P("dp", "tensor"),
            P(),
            P(),
            P(),
            P(),
            P(),
            P(),
            P(),
            P(),
            P(),
        ),
        out_specs=(
            P(("dp", "tensor"), None),
            P(("dp", "tensor"), None),
            P("dp", None, "tensor"),
            P("dp", "tensor"),
            P("dp", "tensor"),
            P("dp", "tensor"),
            P(),
            P(),
            P(),
            P("dp", None, "tensor"),
            P("dp", "tensor"),
            P("dp", "tensor"),
            P("dp", "tensor"),
            P(),
            P(),
            P(),
            P("dp", None, "tensor"),
            P("dp", "tensor"),
            P("dp", "tensor"),
            P("dp", "tensor"),
            P("dp", None, "tensor"),
            P("dp", "tensor"),
            P("dp", "tensor"),
            P("dp", "tensor"),
            P(),
            P(),
            P(),
            P("dp", None, "tensor"),
            P("dp", "tensor"),
            P("dp", "tensor"),
            P("dp", "tensor"),
            P(),
            P(),
            P(),
            P(),
            P(),
        ),
        check_vma=False,
    )
```

```python
import jax
import jax.numpy as jnp
from jax import lax
from jax.experimental import pallas as pl
from jax.experimental.pallas import tpu as pltpu
from jax.sharding import PartitionSpec as P

HEADS = 16
HEAD = 64
VMEM_LIMIT = 48 * 1024 * 1024

learn_rate = 0.5
gelu_coef = 0.7978845608028654


def norm_forward(values, gain, shift):
    mean = jnp.mean(values, axis=-1, keepdims=True)
    centred = values - mean
    inverse = lax.rsqrt(jnp.mean(centred * centred, axis=-1, keepdims=True) + 1e-05)
    unit = centred * inverse
    return (unit * gain + shift, unit, inverse)


def norm_backward(grad, unit, inverse, gain):
    scaled = grad * gain
    inner = (
        scaled
        - jnp.mean(scaled, axis=-1, keepdims=True)
        - unit * jnp.mean(scaled * unit, axis=-1, keepdims=True)
    )
    return (inverse * inner, jnp.sum(grad * unit, axis=0), jnp.sum(grad, axis=0))


def alibi_slopes():
    return jnp.exp2(-8.0 * (lax.iota(jnp.int32, HEADS) + 1).astype(jnp.float32) / HEADS)


def vmem():
    return pl.BlockSpec(memory_space=pltpu.VMEM)


def hbm():
    return pl.BlockSpec(memory_space=pl.ANY)


def smem():
    return pl.BlockSpec(memory_space=pltpu.SMEM)


def shaped(*shape, dtype=jnp.bfloat16):
    return jax.ShapeDtypeStruct(shape, dtype)


def run_kernel(body, operands, in_specs, outs, out_specs, scratch, flops, moved, name):
    return pl.pallas_call(
        body,
        out_shape=outs,
        in_specs=in_specs,
        out_specs=out_specs,
        scratch_shapes=scratch,
        compiler_params=pltpu.CompilerParams(vmem_limit_bytes=VMEM_LIMIT),
        cost_estimate=pl.CostEstimate(flops=flops, bytes_accessed=moved, transcendentals=0),
        name=name,
    )(*operands)


def dot(a, b, contract=(1, 0)):
    return lax.dot_general(
        a, b, (((contract[0],), (contract[1],)), ((), ())), preferred_element_type=jnp.float32
    )


def load_pieces(pieces, target, sems, me, columns=None):
    rows = pieces[0].shape[0]
    copies = []
    for rel, piece in enumerate(pieces):
        source = piece if columns is None else piece.at[:, columns]
        spot = pl.ds(pl.multiple_of((me ^ rel) * rows, rows), rows)
        copies.append(pltpu.make_async_copy(source, target.at[spot], sems.at[rel]))
    for copy in copies:
        copy.start()
    return copies


def store_pieces(source, outs, sems, me, split):
    high, low = split
    rows = source.shape[0] // (high * low)
    copies = []
    for minor in range(low):
        for major in range(high):
            rel = major * low + minor
            spot = pl.ds(pl.multiple_of((me ^ rel) * rows, rows), rows)
            target = outs[minor].at[pl.ds(major * rows, rows)]
            copies.append(pltpu.make_async_copy(source.at[spot], target, sems.at[rel]))
    for copy in copies:
        copy.start()
    for copy in copies:
        copy.wait()


def split_three(v):
    high = v.astype(jnp.bfloat16)
    rest = v - high.astype(jnp.float32)
    middle = rest.astype(jnp.bfloat16)
    return high, middle, (rest - middle.astype(jnp.float32)).astype(jnp.bfloat16)


def widen(part, columns):
    rows = part.shape[0]
    lane = lax.broadcasted_iota(jnp.int32, (rows, HEAD), 1)
    extra = jnp.zeros((rows, HEAD), jnp.float32)
    for spot, column in enumerate(columns):
        extra = jnp.where(lane == spot, column, extra)
    return jnp.concatenate([part.astype(jnp.float32), extra], axis=1).astype(jnp.bfloat16)


def score_mask(gap, rows, block_q, block_k, prefix):
    key_spot = lax.broadcasted_iota(jnp.int32, (rows, rows), 0)
    return (gap <= (block_q - block_k) * rows) | (key_spot < prefix - block_k * rows)


def wide_heads(count, rows, heads, rank, slopes, queries, keys, q_wide, k_wide):
    scale = float(HEAD) ** (-0.5)

    def body(block, carry):
        spot = pl.ds(pl.multiple_of(block * rows, rows), rows)
        place = lax.broadcasted_iota(jnp.int32, (rows, 1), 0) + (rank ^ block) * rows
        q_all, k_all = queries[spot, :], keys[spot, :]
        for head in range(heads):
            part = slice(head * HEAD, (head + 1) * HEAD)
            q_head = q_all[:, part].astype(jnp.float32) * scale
            q_wide[head, spot, :] = widen(q_head, (1.0, 1.0, 1.0))
            lift = split_three(place.astype(jnp.float32) * slopes[head])
            k_wide[head, spot, :] = widen(k_all[:, part], [v.astype(jnp.float32) for v in lift])
        return carry

    lax.fori_loop(0, count, body, 0)


def attend_kernel(count, heads, pieces_count, refs):
    numbers, slopes = refs[0], refs[1]
    normed = refs[2 : 2 + count]
    pieces = refs[2 + count : 2 + count + pieces_count]
    q_shift, v_shift, queries, keys, values, context, logsum = refs[2 + count + pieces_count :][:7]
    partial = refs[9 + count + pieces_count :][:count]
    weights, q_wide, k_wide, v_flip, total, peak, mass, sems = refs[9 + 2 * count + pieces_count :]
    me, rank, prefix = numbers[0], numbers[1], numbers[2]
    rows = normed[0].shape[0]
    width = heads * HEAD
    for copy in load_pieces(pieces, weights, sems, me):
        copy.wait()
    for block in range(count):
        spot = slice(block * rows, (block + 1) * rows)
        made = dot(normed[block][...], weights[:, : 3 * width])
        queries[spot, :] = (made[:, :width] + q_shift[...]).astype(jnp.bfloat16)
        keys[spot, :] = made[:, width : 2 * width].astype(jnp.bfloat16)
        value = made[:, 2 * width :] + v_shift[...]
        values[spot, :] = value.astype(jnp.bfloat16)
        v_flip[:, spot] = value.T.astype(jnp.bfloat16)
    wide_heads(count, rows, heads, rank, slopes, queries, keys, q_wide, k_wide)
    gap = lax.broadcasted_iota(jnp.int32, (rows, rows), 0) - lax.broadcasted_iota(
        jnp.int32, (rows, rows), 1
    )

    def query_block(block, carry):
        own = pl.ds(pl.multiple_of(block * rows, rows), rows)
        peak[...] = jnp.full(peak.shape, -1e30, jnp.float32)
        mass[...] = jnp.zeros(mass.shape, jnp.float32)
        total[...] = jnp.zeros(total.shape, jnp.float32)

        def key_block(other, inner):
            block_q, block_k = rank ^ block, rank ^ other
            spot = pl.ds(pl.multiple_of(other * rows, rows), rows)

            @pl.when((block_k <= block_q) | (block_k * rows < prefix))
            def _():
                allowed = score_mask(gap, rows, block_q, block_k, prefix)
                for head in range(heads):
                    part = slice(head * HEAD, (head + 1) * HEAD)
                    scores = dot(k_wide[head, spot, :], q_wide[head, own, :], (1, 1))
                    scores = jnp.where(allowed, scores, -1e30)
                    before = peak[head : head + 1, :]
                    after = jnp.maximum(before, jnp.max(scores, axis=0, keepdims=True))
                    shrink = jnp.exp(before - after)
                    expo = jnp.exp(scores - after)
                    mass[head : head + 1, :] = mass[head : head + 1, :] * shrink + jnp.sum(
                        expo, axis=0, keepdims=True
                    )
                    peak[head : head + 1, :] = after
                    total[part, :] = total[part, :] * shrink + dot(
                        v_flip[part, spot], expo.astype(jnp.bfloat16)
                    )

            return inner

        lax.fori_loop(0, count, key_block, 0)
        for head in range(heads):
            part = slice(head * HEAD, (head + 1) * HEAD)
            sums = mass[head : head + 1, :]
            total[part, :] = total[part, :] / sums
            logsum[head : head + 1, own] = peak[head : head + 1, :] + jnp.log(sums)
        context[own, :] = total[...].T.astype(jnp.bfloat16)
        return carry

    lax.fori_loop(0, count, query_block, 0)
    for block in range(count):
        spot = slice(block * rows, (block + 1) * rows)
        partial[block][...] = dot(context[spot, :], weights[:, 3 * width :], (1, 1)).astype(
            jnp.bfloat16
        )


def attend(numbers, slopes, normed, pieces, q_shift, v_shift, heads):
    count, parts = len(normed), len(pieces)
    rows, features = normed[0].shape
    width, length = heads * HEAD, rows * count
    outs = [shaped(length, width)] * 4 + [shaped(heads, length, dtype=jnp.float32)]
    outs += [shaped(rows, features)] * count
    scratch = [
        pltpu.VMEM((features, 4 * width), jnp.bfloat16),
        pltpu.VMEM((heads, length, 2 * HEAD), jnp.bfloat16),
        pltpu.VMEM((heads, length, 2 * HEAD), jnp.bfloat16),
        pltpu.VMEM((width, length), jnp.bfloat16),
        pltpu.VMEM((width, rows), jnp.float32),
        pltpu.VMEM((heads, rows), jnp.float32),
        pltpu.VMEM((heads, rows), jnp.float32),
        pltpu.SemaphoreType.DMA((parts,)),
    ]
    result = run_kernel(
        lambda *refs: attend_kernel(count, heads, parts, refs),
        (numbers, slopes, *normed, *pieces, q_shift, v_shift),
        [smem(), smem()] + [vmem()] * count + [hbm()] * parts + [vmem()] * 2,
        outs,
        [vmem()] * len(outs),
        scratch,
        2 * length * features * 4 * width + 4 * length * length * width,
        2 * length * (2 * features + 4 * width) + 8 * features * width,
        "attend",
    )
    return result[:5], result[5:]


def attend_back_kernel(count, heads, pieces_count, refs):
    numbers, slopes, queries, keys, values, context, logsum = refs[:7]
    branch = refs[7 : 7 + count]
    pieces = refs[7 + count : 7 + count + pieces_count]
    stacked, sums = refs[7 + count + pieces_count :][:2]
    partial = refs[9 + count + pieces_count :][:count]
    weights, q_wide, k_wide, g_wide, v_wide, k_flip, dk, dv, dq, sems = refs[
        9 + 2 * count + pieces_count :
    ]
    me, rank, prefix = numbers[0], numbers[1], numbers[2]
    rows = branch[0].shape[0]
    width = heads * HEAD
    scale = float(HEAD) ** (-0.5)
    copies = load_pieces(pieces, weights, sems, me)
    wide_heads(count, rows, heads, rank, slopes, queries, keys, q_wide, k_wide)
    for copy in copies:
        copy.wait()
    for block in range(count):
        spot = slice(block * rows, (block + 1) * rows)
        grad = dot(branch[block][...], weights[:, 3 * width :]).astype(jnp.bfloat16)
        grad = grad.astype(jnp.float32)
        inner = grad * context[spot, :].astype(jnp.float32)
        k_flip[:, spot] = keys[spot, :].astype(jnp.float32).T.astype(jnp.bfloat16)
        for head in range(heads):
            part = slice(head * HEAD, (head + 1) * HEAD)
            delta = -jnp.sum(inner[:, part], axis=1, keepdims=True)
            lift = [v.astype(jnp.float32) for v in split_three(delta)]
            g_wide[head, spot, :] = widen(grad[:, part], lift)
            v_wide[head, spot, :] = widen(values[spot, part], (1.0, 1.0, 1.0))
    dk[...] = jnp.zeros(dk.shape, jnp.float32)
    dv[...] = jnp.zeros(dv.shape, jnp.float32)
    gap = lax.broadcasted_iota(jnp.int32, (rows, rows), 0) - lax.broadcasted_iota(
        jnp.int32, (rows, rows), 1
    )

    def query_block(block, carry):
        own = pl.ds(pl.multiple_of(block * rows, rows), rows)
        dq[...] = jnp.zeros(dq.shape, jnp.float32)

        def key_block(other, inner):
            block_q, block_k = rank ^ block, rank ^ other
            spot = pl.ds(pl.multiple_of(other * rows, rows), rows)

            @pl.when((block_k <= block_q) | (block_k * rows < prefix))
            def _():
                allowed = score_mask(gap, rows, block_q, block_k, prefix)
                for head in range(heads):
                    part = slice(head * HEAD, (head + 1) * HEAD)
                    q_part, g_part = q_wide[head, own, :], g_wide[head, own, :]
                    scores = dot(k_wide[head, spot, :], q_part, (1, 1))
                    scores = scores - logsum[head : head + 1, own]
                    probs = jnp.exp(jnp.where(allowed, scores, -1e30))
                    change = dot(v_wide[head, spot, :], g_part, (1, 1))
                    low = (probs * change).astype(jnp.bfloat16)
                    dv[head, spot, :] += dot(probs.astype(jnp.bfloat16), g_part)
                    dk[head, spot, :] += dot(low, q_part)
                    dq[part, :] += dot(k_flip[part, spot], low)

            return inner

        lax.fori_loop(0, count, key_block, 0)
        stacked[own, :width] = (dq[...].T * scale).astype(jnp.bfloat16)
        return carry

    lax.fori_loop(0, count, query_block, 0)
    sums[...] = jnp.zeros(sums.shape, jnp.float32)
    for block in range(count):
        spot = slice(block * rows, (block + 1) * rows)
        for start, source in ((width, dk), (2 * width, dv)):
            made = [source[head, spot, :HEAD] for head in range(heads)]
            made = jnp.concatenate(made, axis=1).astype(jnp.bfloat16)
            stacked[spot, start : start + width] = made
        whole = stacked[spot, :]
        sums[...] += jnp.sum(whole.astype(jnp.float32), axis=0, keepdims=True)
        partial[block][...] = dot(whole, weights[:, : 3 * width], (1, 1)).astype(jnp.bfloat16)


def attend_back(numbers, slopes, saved, branch, pieces, heads):
    count, parts = len(branch), len(pieces)
    rows, features = branch[0].shape
    width, length = heads * HEAD, rows * count
    outs = [shaped(length, 3 * width), shaped(1, 3 * width, dtype=jnp.float32)]
    outs += [shaped(rows, features)] * count
    wide = pltpu.VMEM((heads, length, 2 * HEAD), jnp.bfloat16)
    scratch = [pltpu.VMEM((features, 4 * width), jnp.bfloat16), wide, wide, wide, wide]
    scratch += [
        pltpu.VMEM((width, length), jnp.bfloat16),
        pltpu.VMEM((heads, length, 2 * HEAD), jnp.float32),
        pltpu.VMEM((heads, length, 2 * HEAD), jnp.float32),
        pltpu.VMEM((width, rows), jnp.float32),
        pltpu.SemaphoreType.DMA((parts,)),
    ]
    result = run_kernel(
        lambda *refs: attend_back_kernel(count, heads, parts, refs),
        (numbers, slopes, *saved, *branch, *pieces),
        [smem(), smem()] + [vmem()] * (5 + count) + [hbm()] * parts,
        outs,
        [vmem()] * len(outs),
        scratch,
        2 * length * features * 4 * width + 10 * length * length * width,
        2 * length * (2 * features + 7 * width) + 8 * features * width,
        "attend_back",
    )
    return result[0], result[1], result[2:]


def gelu_both(v):
    square = v * v
    hyper = jnp.tanh(gelu_coef * (v + 0.044715 * square * v))
    half = 0.5 * (1.0 + hyper)
    slope = half + 0.5 * v * (1.0 - hyper * hyper) * (
        gelu_coef + gelu_coef * 3.0 * 0.044715 * square
    )
    return v * half, slope


def feed_kernel(count, pieces_count, refs):
    numbers = refs[0]
    two, cot = refs[1 : 1 + count], refs[1 + count : 1 + 2 * count]
    pieces = refs[1 + 2 * count : 1 + 2 * count + pieces_count]
    shift, hidden, grads, sums = refs[1 + 2 * count + pieces_count :][:4]
    partial = refs[5 + 2 * count + pieces_count :][:count]
    weights, sems = refs[5 + 3 * count + pieces_count :]
    rows = two[0].shape[0]
    inner = shift.shape[1]
    for copy in load_pieces(pieces, weights, sems, numbers[0]):
        copy.wait()
    sums[...] = jnp.zeros(sums.shape, jnp.float32)
    for block in range(count):
        spot = slice(block * rows, (block + 1) * rows)
        pre = dot(two[block][...], weights[:, :inner]) + shift[...]
        value, slope = gelu_both(pre)
        hidden[spot, :] = value.astype(jnp.bfloat16)
        grad = (dot(cot[block][...], weights[:, inner:]) * slope).astype(jnp.bfloat16)
        grads[spot, :] = grad
        sums[...] += jnp.sum(grad.astype(jnp.float32), axis=0, keepdims=True)
        partial[block][...] = dot(grad, weights[:, :inner], (1, 1)).astype(jnp.bfloat16)


def feed(numbers, two, cot, pieces, shift):
    count, parts = len(two), len(pieces)
    rows, features = two[0].shape
    inner = shift.shape[1]
    outs = [shaped(rows * count, inner)] * 2 + [shaped(1, inner, dtype=jnp.float32)]
    outs += [shaped(rows, features)] * count
    result = run_kernel(
        lambda *refs: feed_kernel(count, parts, refs),
        (numbers, *two, *cot, *pieces, shift),
        [smem()] + [vmem()] * (2 * count) + [hbm()] * parts + [vmem()],
        outs,
        [vmem()] * len(outs),
        [
            pltpu.VMEM((features, 2 * inner), jnp.bfloat16),
            pltpu.SemaphoreType.DMA((parts,)),
        ],
        6 * rows * count * features * inner,
        4 * rows * count * (features + inner) + 4 * features * inner,
        "feed",
    )
    return result[0], result[1], result[2], result[3:]


def down_kernel(count, pieces_count, refs):
    numbers, hidden = refs[0], refs[1 : 1 + count // 2]
    pieces = refs[1 + count // 2 : 1 + count // 2 + pieces_count]
    partial = refs[1 + count // 2 + pieces_count :][:count]
    weights, sems = refs[1 + count // 2 + pieces_count + count :]
    inner = weights.shape[1]
    rows = partial[0].shape[0]
    columns = pl.ds(pieces[0].shape[1] - inner, inner)
    for copy in load_pieces(pieces, weights, sems, numbers[0], columns):
        copy.wait()
    for block in range(count):
        spot = slice((block % 2) * rows, (block % 2 + 1) * rows)
        partial[block][...] = dot(hidden[block // 2][spot, :], weights[...], (1, 1)).astype(
            jnp.bfloat16
        )


def down(numbers, hidden, pieces, features):
    parts, count = len(pieces), 2 * len(hidden)
    rows, inner = hidden[0].shape[0] // 2, hidden[0].shape[1]
    return run_kernel(
        lambda *refs: down_kernel(count, parts, refs),
        (numbers, *hidden, *pieces),
        [smem()] + [vmem()] * len(hidden) + [hbm()] * parts,
        [shaped(rows, features)] * count,
        [vmem()] * count,
        [pltpu.VMEM((features, inner), jnp.bfloat16), pltpu.SemaphoreType.DMA((parts,))],
        2 * rows * count * features * inner,
        2 * rows * count * (features + inner) + 2 * features * inner,
        "down",
    )


def grads_kernel(pairs, split, refs):
    numbers = refs[0]
    at = 1
    made, start = refs[-2], 0
    for left_count, right_count in pairs:
        left, right = refs[at : at + left_count], refs[at + left_count :][:right_count]
        at += left_count + right_count
        width = right[0].shape[1]
        tall = jnp.concatenate([v[...] for v in left], axis=0)
        wide = jnp.concatenate([v[...] for v in right], axis=0)
        made[:, start : start + width] = dot(tall, wide, (0, 0)).astype(jnp.bfloat16)
        start += width
    store_pieces(made, refs[at : at + split[1]], refs[-1], numbers[0], split)


def weight_grads(numbers, pairs, split):
    features = pairs[0][0][0].shape[1]
    rows = sum(v.shape[0] for v in pairs[0][0])
    width = sum(right[0].shape[1] for left, right in pairs)
    operands = [v for left, right in pairs for v in (*left, *right)]
    counts = [(len(left), len(right)) for left, right in pairs]
    return run_kernel(
        lambda *refs: grads_kernel(counts, split, refs),
        (numbers, *operands),
        [smem()] + [vmem()] * len(operands),
        [shaped(features // split[1], width)] * split[1],
        [hbm()] * split[1],
        [
            pltpu.VMEM((features, width), jnp.bfloat16),
            pltpu.SemaphoreType.DMA((split[0] * split[1],)),
        ],
        2 * rows * features * width,
        2 * rows * (features + width) + 2 * features * width,
        "weight_grads",
    )


def norm_kernel(*refs):
    base, parts, (shift, gain, offset, resid, normed) = refs[0], refs[1:-5], refs[-5:]
    total = base[...].astype(jnp.float32)
    if parts:
        total = total + (sum(v[...].astype(jnp.float32) for v in parts) + shift[...])
    resid[...] = total
    normed[...] = norm_forward(total, gain[...], offset[...])[0].astype(jnp.bfloat16)


def norm(base, parts, shift, gain, offset):
    rows, features = base.shape
    operands = (base, *parts, shift, gain, offset)
    return run_kernel(
        norm_kernel,
        operands,
        [vmem()] * len(operands),
        [shaped(rows, features, dtype=jnp.float32), shaped(rows, features)],
        [vmem()] * 2,
        [],
        10 * rows * features,
        rows * features * (8 + 2 * len(parts)),
        "norm",
    )


def norm_back_kernel(with_branch, refs):
    values, gain, residual = refs[:3]
    parts = refs[3 : -3 if with_branch else -2]
    grad = sum(v[...].astype(jnp.float32) for v in parts)
    _, unit, inverse = norm_forward(values[...].astype(jnp.float32), 1.0, 0.0)
    change, gain_grad, shift_grad = norm_backward(grad, unit, inverse, gain[...])
    before = residual[...].astype(jnp.float32)
    total = before + change
    made, sums = (refs[-3], refs[-1]) if with_branch else refs[-2:]
    made[...] = total
    lines = [gain_grad[None], shift_grad[None]]
    if with_branch:
        low = total.astype(jnp.bfloat16)
        refs[-2][...] = low
        lines.append(jnp.sum(low.astype(jnp.float32), axis=0, keepdims=True))
        lines.append(jnp.sum(before, axis=0, keepdims=True))
    for spot, line in enumerate(lines):
        sums[spot : spot + 1, :] = line


def norm_back(values, gain, residual, parts, with_branch):
    rows, features = values.shape
    operands = (values, gain, residual, *parts)
    outs = [shaped(rows, features, dtype=jnp.float32)]
    outs += [shaped(rows, features)] if with_branch else []
    outs += [shaped(4 if with_branch else 2, features, dtype=jnp.float32)]
    return run_kernel(
        lambda *refs: norm_back_kernel(with_branch, refs),
        operands,
        [vmem()] * len(operands),
        outs,
        [vmem()] * len(outs),
        [],
        20 * rows * features,
        rows * features * (10 + 2 * len(parts)),
        "norm_back",
    )


def swap(v, axis, rel):
    return lax.ppermute(v, axis, [(i, i ^ rel) for i in range(lax.axis_size(axis))])


def dp_split():
    bits = lax.axis_size("dp").bit_length() - 1
    low = 1 << ((bits - 1) // 2)
    return lax.axis_size("dp") // low, low


def gather_pieces(shard):
    high, low = dp_split()
    pieces = {0: shard}
    for major in range(1, high):
        pieces[major * low] = swap(shard, "dp", major * low)
    for minor in range(1, low):
        for major in range(high):
            pieces[major * low + minor] = swap(pieces[major * low], "dp", minor)
    return [pieces[rel] for rel in range(high * low)]


def scatter_rows(parts):
    high, low = dp_split()
    rows = parts[0].shape[0] // high
    total = parts[0].astype(jnp.float32)
    for minor in range(1, low):
        total = total + swap(parts[minor], "dp", minor).astype(jnp.float32)
    result = total[:rows]
    for major in range(1, high):
        block = total[major * rows : (major + 1) * rows].astype(jnp.bfloat16)
        result = result + swap(block, "dp", major * low).astype(jnp.float32)
    return result


def share_rows(own):
    count = lax.axis_size("tensor")
    pieces = {0: own, 1: swap(own, "tensor", 1)}
    for rel in range(2, count, 2):
        pieces[rel] = swap(own, "tensor", rel)
        pieces[rel + 1] = swap(pieces[rel], "tensor", 1)
    return [pieces[rel] for rel in range(count)]


def collect_rows(blocks):
    parts = [blocks[0]]
    for rel in range(2, len(blocks), 2):
        other = swap(blocks[rel + 1], "tensor", 1).astype(jnp.float32)
        joined = (blocks[rel].astype(jnp.float32) + other).astype(jnp.bfloat16)
        parts.append(swap(joined, "tensor", rel))
    return parts + [swap(blocks[1], "tensor", 1)]


def sum_everywhere(v):
    for axis in ("tensor", "dp"):
        total = v
        for rel in range(1, lax.axis_size(axis)):
            total = total + swap(v, axis, rel)
        v = total
    return v


def sum_in_steps(v):
    for axis in ("tensor", "dp"):
        rel = 1
        while rel < lax.axis_size(axis):
            v = v + swap(v, axis, rel)
            rel *= 2
    return v


def lines(values):
    spot = lax.iota(jnp.int32, len(values))
    made = jnp.broadcast_to(values[0], spot.shape)
    for at in range(1, len(values)):
        made = jnp.where(spot == at, values[at], made)
    return made


def place(part, width, rank):
    return lax.dynamic_update_slice(jnp.zeros((width,), jnp.float32), part, (rank * part.shape[0],))


def adam_terms(moment, square, grad):
    new_moment = 0.5 * moment + 0.5 * grad
    new_square = 0.5 * square + 0.5 * grad * grad
    return (new_moment, new_square, new_moment / (jnp.sqrt(new_square) + 1e-06))


def lamb_rows(weight, moment, square, grad):
    new_moment, new_square, direction = adam_terms(moment, square, grad)
    weight_norm = jnp.sqrt(jnp.sum(weight * weight, axis=-1, keepdims=True))
    step_norm = jnp.sqrt(jnp.sum(direction * direction, axis=-1, keepdims=True))
    return (weight - learn_rate * (weight_norm / step_norm) * direction, new_moment, new_square)


def per_device(
    tokens,
    cotangent,
    prefix,
    qkv_weight,
    qkv_moment,
    qkv_square,
    out_weight,
    out_moment,
    out_square,
    up_weight,
    up_moment,
    up_square,
    down_weight,
    down_moment,
    down_square,
    norm_gains,
    gains_moment,
    gains_square,
    biases,
    biases_moment,
    biases_square,
    up_bias,
    up_bias_moment,
    up_bias_square,
):
    rows, width = tokens.shape
    count = lax.axis_size("tensor")
    rank = lax.axis_index("tensor")
    me = lax.axis_index("dp")
    split = dp_split()
    local_width = qkv_weight.shape[2]
    local_hidden = up_weight.shape[1]
    heads_here = local_width // HEAD
    slopes = lax.dynamic_slice_in_dim(alibi_slopes(), rank * heads_here, heads_here)
    numbers = lines([me, rank, prefix[0]])
    line = lambda v: v[None]
    own_columns = lambda v, size: lax.dynamic_slice_in_dim(v, rank * size, size)[None]
    mix_shard = jnp.concatenate([qkv_weight[:, kind] for kind in range(3)] + [out_weight], axis=1)
    feed_shard = jnp.concatenate([up_weight, down_weight], axis=1)
    mix_pieces = gather_pieces(mix_shard.astype(jnp.bfloat16))
    _, normed = norm(tokens, (), line(biases[4]), line(norm_gains[0]), line(biases[0]))
    normed_blocks = share_rows(normed)
    feed_pieces = gather_pieces(feed_shard.astype(jnp.bfloat16))
    cot_blocks = share_rows(cotangent)
    saved, attn_blocks = attend(
        numbers,
        slopes,
        normed_blocks,
        mix_pieces,
        own_columns(biases[2], local_width),
        own_columns(biases[3], local_width),
        heads_here,
    )
    resid, normed_two = norm(
        tokens,
        collect_rows(attn_blocks),
        line(biases[4]),
        line(norm_gains[1]),
        line(biases[1]),
    )
    two_blocks = share_rows(normed_two)
    up_slice = own_columns(up_bias, local_hidden)
    hidden, pre_grads, two_grads, up_bias_sum = [], [], [], 0.0
    for start in range(0, count, 2):
        made = feed(
            numbers,
            two_blocks[start : start + 2],
            cot_blocks[start : start + 2],
            feed_pieces,
            up_slice,
        )
        hidden.append(made[0])
        pre_grads.append(made[1])
        up_bias_sum = up_bias_sum + made[2]
        two_grads.extend(made[3])
    two_parts = collect_rows(two_grads)
    down_g = scatter_rows(weight_grads(numbers, [(cot_blocks, hidden)], split))
    up_g = scatter_rows(weight_grads(numbers, [(two_blocks, pre_grads)], split))
    mlp_parts = collect_rows(down(numbers, hidden, feed_pieces, width))
    mlp_rows = sum(v.astype(jnp.float32) for v in mlp_parts)
    output = (resid + (mlp_rows + biases[5])).astype(jnp.bfloat16)
    resid_grad, branch_low, two_sums = norm_back(
        resid, line(norm_gains[1]), cotangent, two_parts, True
    )
    branch_blocks = share_rows(branch_low)
    stacked, head_sums, one_blocks = attend_back(
        numbers, slopes, saved, branch_blocks, mix_pieces, heads_here
    )
    one_parts = collect_rows(one_blocks)
    mix_g = scatter_rows(
        weight_grads(
            numbers, [(normed_blocks, [stacked]), (branch_blocks, [saved[3]])], split
        )
    )
    qkv_g = mix_g[:, : 3 * local_width].reshape(qkv_weight.shape)
    out_g = mix_g[:, 3 * local_width :]
    input_grad, one_sums = norm_back(tokens, line(norm_gains[0]), resid_grad, one_parts, False)
    small = jnp.concatenate(
        [
            one_sums.reshape(-1),
            two_sums.reshape(-1),
            place(head_sums[0, :local_width], width, rank),
            place(head_sums[0, 2 * local_width :], width, rank),
            place(up_bias_sum[0], up_bias.shape[0], rank),
        ]
    )
    small = sum_in_steps(small.reshape(-1, width))
    gains_g = jnp.concatenate([small[0:1], small[2:3]], axis=0)
    biases_g = jnp.concatenate([small[1:2], small[3:4], small[6:8], small[4:6]], axis=0)
    upb_g = small[8:].reshape(-1)
    qkv_m, qkv_s, qkv_dir = adam_terms(qkv_moment, qkv_square, qkv_g)
    out_m, out_s, out_dir = adam_terms(out_moment, out_square, out_g)
    up_m, up_s, up_dir = adam_terms(up_moment, up_square, up_g)
    down_m, down_s, down_dir = adam_terms(down_moment, down_square, down_g)
    local_sums = lines(
        [
            jnp.sum(qkv_weight * qkv_weight),
            jnp.sum(qkv_dir * qkv_dir),
            jnp.sum(out_weight * out_weight),
            jnp.sum(out_dir * out_dir),
            jnp.sum(up_weight * up_weight),
            jnp.sum(up_dir * up_dir),
            jnp.sum(down_weight * down_weight),
            jnp.sum(down_dir * down_dir),
        ]
    )
    totals = sum_everywhere(local_sums)
    norms = jnp.sqrt(totals).reshape(4, 2)
    qkv_n = qkv_weight - learn_rate * (norms[0, 0] / norms[0, 1]) * qkv_dir
    out_n = out_weight - learn_rate * (norms[1, 0] / norms[1, 1]) * out_dir
    up_n = up_weight - learn_rate * (norms[2, 0] / norms[2, 1]) * up_dir
    down_n = down_weight - learn_rate * (norms[3, 0] / norms[3, 1]) * down_dir
    gains_n, gains_m, gains_s = lamb_rows(norm_gains, gains_moment, gains_square, gains_g)
    biases_n, biases_m, biases_s = lamb_rows(biases, biases_moment, biases_square, biases_g)
    upb_n, upb_m, upb_s = lamb_rows(up_bias, up_bias_moment, up_bias_square, upb_g)
    return (
        output,
        input_grad,
        qkv_g,
        out_g,
        up_g,
        down_g,
        gains_g,
        biases_g,
        upb_g,
        qkv_n,
        out_n,
        up_n,
        down_n,
        gains_n,
        biases_n,
        upb_n,
        qkv_n.astype(jnp.bfloat16),
        out_n.astype(jnp.bfloat16),
        up_n.astype(jnp.bfloat16),
        down_n.astype(jnp.bfloat16),
        qkv_m,
        out_m,
        up_m,
        down_m,
        gains_m,
        biases_m,
        upb_m,
        qkv_s,
        out_s,
        up_s,
        down_s,
        gains_s,
        biases_s,
        upb_s,
        norms[:, 0],
        norms[:, 1],
    )


def solution(mesh):
    return jax.shard_map(
        per_device,
        mesh=mesh,
        in_specs=(
            P(("dp", "tensor"), None),
            P(("dp", "tensor"), None),
            P("dp"),
            P("dp", None, "tensor"),
            P("dp", None, "tensor"),
            P("dp", None, "tensor"),
            P("dp", "tensor"),
            P("dp", "tensor"),
            P("dp", "tensor"),
            P("dp", "tensor"),
            P("dp", "tensor"),
            P("dp", "tensor"),
            P("dp", "tensor"),
            P("dp", "tensor"),
            P("dp", "tensor"),
            P(),
            P(),
            P(),
            P(),
            P(),
            P(),
            P(),
            P(),
            P(),
        ),
        out_specs=(
            P(("dp", "tensor"), None),
            P(("dp", "tensor"), None),
            P("dp", None, "tensor"),
            P("dp", "tensor"),
            P("dp", "tensor"),
            P("dp", "tensor"),
            P(),
            P(),
            P(),
            P("dp", None, "tensor"),
            P("dp", "tensor"),
            P("dp", "tensor"),
            P("dp", "tensor"),
            P(),
            P(),
            P(),
            P("dp", None, "tensor"),
            P("dp", "tensor"),
            P("dp", "tensor"),
            P("dp", "tensor"),
            P("dp", None, "tensor"),
            P("dp", "tensor"),
            P("dp", "tensor"),
            P("dp", "tensor"),
            P(),
            P(),
            P(),
            P("dp", None, "tensor"),
            P("dp", "tensor"),
            P("dp", "tensor"),
            P("dp", "tensor"),
            P(),
            P(),
            P(),
            P(),
            P(),
        ),
        check_vma=False,
    )
```
